32 devices in a mesh: seq: 4 (over y, core), fsdp: 8 (over z, x).
Axes of the slice: x: 2, y: 2, z: 4, core: 2. Of those that a mesh axis runs over, the one named last changes fastest.
Arguments:
- activations: float32 [8, 28, 42, 512], P('fsdp', 'seq'), may hold values from -6 to 6
- first_gain: float32 [2, 512], P(None, 'fsdp'), may hold values from 0.5 to 1.5
- first_offset: float32 [2, 512], P(None, 'fsdp'), may hold values from -3 to 3
- attend_weight: bfloat16 [2, 512, 1536], P(None, 'fsdp'), may hold values from -0.25 to 0.25
- query_bias: float32 [2, 512], P(None, 'fsdp'), may hold values from -3 to 3
- value_bias: float32 [2, 512], P(None, 'fsdp'), may hold values from -3 to 3
- output_weight: bfloat16 [2, 512, 512], P(None, 'fsdp'), may hold values from -1.5 to 1.5
- output_bias: float32 [2, 512], P(None, 'fsdp'), may hold values from -1.75 to 1.75
- second_gain: float32 [2, 512], P(None, 'fsdp'), may hold values from 0.5 to 1.5
- second_offset: float32 [2, 512], P(None, 'fsdp'), may hold values from -3 to 3
- expand_weight: bfloat16 [2, 512, 2048], P(None, 'fsdp'), may hold values from -0.25 to 0.25
- expand_bias: float32 [2, 2048], P(None, 'fsdp'), may hold values from -3 to 3
- reduce_weight: bfloat16 [2, 2048, 512], P(None, 'fsdp'), may hold values from -0.125 to 0.125
- reduce_bias: float32 [2, 512], P(None, 'fsdp'), may hold values from -1.75 to 1.75
- position_table: float32 [2, 169, 16], replicated, may hold values from -6 to 6
- table_index: int32 [49, 49], replicated, may hold values from 0 to 168, as said below
- cotangent: float32 [8, 28, 42, 512], P('fsdp', 'seq'), may hold values from -6 to 6
Outputs:
- block_output: float32 [8, 28, 42, 512], P('fsdp', 'seq')
- input_grad: float32 [8, 28, 42, 512], P('fsdp', 'seq')
- grad_first_gain: float32 [2, 512], P(None, 'fsdp')
- grad_first_offset: float32 [2, 512], P(None, 'fsdp')
- grad_attend_weight: float32 [2, 512, 1536], P(None, 'fsdp')
- grad_query_bias: float32 [2, 512], P(None, 'fsdp')
- grad_value_bias: float32 [2, 512], P(None, 'fsdp')
- grad_output_weight: float32 [2, 512, 512], P(None, 'fsdp')
- grad_output_bias: float32 [2, 512], P(None, 'fsdp')
- grad_second_gain: float32 [2, 512], P(None, 'fsdp')
- grad_second_offset: float32 [2, 512], P(None, 'fsdp')
- grad_expand_weight: float32 [2, 512, 2048], P(None, 'fsdp')
- grad_expand_bias: float32 [2, 2048], P(None, 'fsdp')
- grad_reduce_weight: float32 [2, 2048, 512], P(None, 'fsdp')
- grad_reduce_bias: float32 [2, 512], P(None, 'fsdp')
- grad_position_table: float32 [2, 169, 16], replicated
The draws below stay inside these ranges and needn't reach their ends.
Inputs may be any that keep to these rules, and one draw needn't show every extreme that they name: table_index[i, j] = perm[(dy + 6) (13) + dx + 6], where dy, dx are the row and column offsets of window position i from position j and perm is a permutation of the table rows.
All inputs are finite; a program needn't handle non-finite values.
Results may differ from the reference program's by a relative error of at most 0.035.
Values may be sent and summed in bfloat16 or wider, within the bound.
No kernel may reach another device: no remote copies, remote signals or barrier semaphores. Data moves between devices by JAX's collectives and lax.ppermute only.
A program may use at most 192 MiB of HBM per device.

```python
import math
import jax
import jax.numpy as jnp
from jax import lax

HEADS = 16
HEAD = 32
D = 512
MLP = 2048
WIN = 7
SHIFT = 3
COLS = 42
ROWS = 28
IMAGES = 8
TABLE = 169


def draw_table_index(key, part):
    order = jax.random.permutation(jax.random.fold_in(key, 11), TABLE).astype(jnp.int32)
    places = jnp.arange(WIN * WIN, dtype=jnp.int32)
    row_pos = places // WIN
    col_pos = places % WIN
    offset_rows = row_pos[:, None] - row_pos[None, :] + (WIN - 1)
    offset_cols = col_pos[:, None] - col_pos[None, :] + (WIN - 1)
    base = offset_rows * (2 * WIN - 1) + offset_cols
    return order[base].astype(jnp.int32)


def steps_of(stream_key, shape, shards, smallest, high):
    def one(dim, shards_of):
        heights = jax.random.uniform(jax.random.fold_in(jax.random.fold_in(stream_key, 6), dim), (shards_of,), jnp.float32, smallest / len(shards), high / len(shards))
        return jnp.repeat(jnp.exp(heights), shape[dim] // shards_of).reshape((-1,) + (1,) * (len(shape) - dim - 1))

    level = one(*shards[0])
    for cut in shards[1:]:
        level = level * one(*cut)
    return level


def normal_values(rng, extent, scale, reach, cuts=(), kind=jnp.bfloat16):
    values = jax.random.normal(rng, extent, jnp.float32) * scale
    if len(cuts) > 0:
        values = steps_of(rng, extent, cuts, -0.22, 0.18) * values
    return jnp.clip(values, min=-reach, max=reach).astype(kind)


def setup_inputs(seed: int = 0) -> dict:
    streams_of = jax.random.split(jax.random.key(seed), 18)
    activations = normal_values(streams_of[0], (IMAGES, ROWS, COLS, D), 1.0, 6.0, ((0, 8), (1, 4)), jnp.float32)
    first_gain = jnp.clip(1.0 + 0.1 * jax.random.normal(streams_of[1], (2, D), jnp.float32), 0.5, 1.5)
    first_offset = normal_values(streams_of[2], (2, D), 0.5, 3.0, ((1, 8),), jnp.float32)
    attend_weight = normal_values(streams_of[3], (2, D, 3 * D), D ** -0.5, 0.25, ((1, 8),))
    query_bias = normal_values(streams_of[4], (2, D), 0.5, 3.0, ((1, 8),), jnp.float32)
    value_bias = normal_values(streams_of[5], (2, D), 0.5, 3.0, ((1, 8),), jnp.float32)
    output_weight = normal_values(streams_of[6], (2, D, D), (max(D // 32, 1)) ** -0.5, 1.5, ((1, 8),))
    output_bias = normal_values(streams_of[7], (2, D), 0.3, 1.75, ((1, 8),), jnp.float32)
    second_gain = jnp.clip(1.0 + 0.1 * jax.random.normal(streams_of[8], (2, D), jnp.float32), 0.5, 1.5)
    second_offset = normal_values(streams_of[9], (2, D), 0.5, 3.0, ((1, 8),), jnp.float32)
    expand_weight = normal_values(streams_of[10], (2, D, MLP), D ** -0.5, 0.25, ((1, 8),))
    expand_bias = normal_values(streams_of[11], (2, MLP), 0.5, 3.0, ((1, 8),), jnp.float32)
    reduce_weight = normal_values(streams_of[12], (2, MLP, D), MLP ** -0.5, 0.125, ((1, 8),))
    reduce_bias = normal_values(streams_of[13], (2, D), 0.3, 1.75, ((1, 8),), jnp.float32)
    position_table = normal_values(streams_of[14], (2, TABLE, HEADS), 1.0, 6.0, (), jnp.float32)
    table_index = draw_table_index(jax.random.fold_in(streams_of[17], 71), 0)
    cotangent = normal_values(streams_of[16], (IMAGES, ROWS, COLS, D), 1.0, 6.0, ((0, 8), (1, 4)), jnp.float32)
    return dict(activations=activations, first_gain=first_gain, first_offset=first_offset, attend_weight=attend_weight, query_bias=query_bias, value_bias=value_bias, output_weight=output_weight, output_bias=output_bias, second_gain=second_gain, second_offset=second_offset, expand_weight=expand_weight, expand_bias=expand_bias, reduce_weight=reduce_weight, reduce_bias=reduce_bias, position_table=position_table, table_index=table_index, cotangent=cotangent)


EPS = 1e-05

def norm_forward(values, gain_vec, offset_vec):
    row_mean = lax.optimization_barrier(jnp.mean(values, -1, keepdims=True))
    centered = values - row_mean
    row_var = lax.optimization_barrier(jnp.mean(centered * centered, -1, keepdims=True))
    inv_std = lax.rsqrt(row_var + EPS)
    normal_x = centered * inv_std
    return (normal_x * gain_vec + offset_vec, normal_x, inv_std)

def norm_backward(upstream, normal_x, inv_std, gain_vec):
    scaled = upstream * gain_vec
    result = inv_std * (scaled - lax.optimization_barrier(jnp.mean(scaled, -1, keepdims=True)) - normal_x * lax.optimization_barrier(jnp.mean(scaled * normal_x, -1, keepdims=True)))
    return (result, lax.optimization_barrier(jnp.sum(upstream * normal_x, 0)), lax.optimization_barrier(jnp.sum(upstream, 0)))

def window_split(grid):
    batch, rows, cols, width = grid.shape
    parted = grid.reshape(batch, rows // WIN, WIN, cols // WIN, WIN, width).transpose(0, 1, 3, 2, 4, 5)
    return parted.reshape(batch * (rows // WIN) * (cols // WIN), WIN * WIN, width)

def window_merge(windows, batch, rows, cols):
    width = windows.shape[-1]
    parted = windows.reshape(batch, rows // WIN, cols // WIN, WIN, WIN, width).transpose(0, 1, 3, 2, 4, 5)
    return parted.reshape(batch, rows, cols, width)

def slice_label(positions, total):
    first = (positions >= total - WIN).astype(jnp.int32)
    second = (positions >= total - SHIFT).astype(jnp.int32)
    return first + second

def region_labels(rows_here, first_row, total_rows, cols):
    row_pos = first_row + jnp.arange(rows_here, dtype=jnp.int32)
    col_pos = jnp.arange(cols, dtype=jnp.int32)
    return slice_label(row_pos, total_rows)[:, None] * 3 + slice_label(col_pos, cols)[None, :]

def region_select(labels):
    rows, cols = labels.shape
    parted = labels.reshape(rows // WIN, WIN, cols // WIN, WIN).transpose(0, 2, 1, 3).reshape(-1, WIN * WIN)
    return (parted[:, :, None] == parted[:, None, :]).astype(jnp.float32)

def score_fn(query_rows, key_rows, rel_bias):
    return jnp.einsum('wihd,wjhd->whij', query_rows.astype(jnp.float32), key_rows.astype(jnp.float32)) + rel_bias[None]

def forward_layer(stream_w, block_parameters, rel_bias, same_region):
    nwin = stream_w.shape[0]
    count = nwin * WIN * WIN
    residual_stream = stream_w.reshape(count, D)
    normalized, first_standardized, first_inverse_deviation = norm_forward(residual_stream, block_parameters[0], block_parameters[1])
    normalized_rows = normalized.astype(jnp.bfloat16)
    projected = jnp.dot(normalized_rows, block_parameters[2], preferred_element_type=jnp.float32)
    scale_factor = 1.0 / math.sqrt(HEAD)
    query_rows = ((projected[:, :D] + block_parameters[3]) * scale_factor).astype(jnp.bfloat16).reshape(nwin, WIN * WIN, HEADS, HEAD)
    key_rows = projected[:, D:2 * D].astype(jnp.bfloat16).reshape(nwin, WIN * WIN, HEADS, HEAD)
    value_rows = (projected[:, 2 * D:] + block_parameters[4]).astype(jnp.bfloat16).reshape(nwin, WIN * WIN, HEADS, HEAD)
    scores = score_fn(query_rows, key_rows, rel_bias)
    exps = jnp.exp(scores)
    if same_region is not None:
        exps = exps * same_region[:, None]
    logsumexp_total = jnp.log(lax.optimization_barrier(jnp.sum(exps, -1, keepdims=True)))
    probs = jnp.exp(scores - logsumexp_total)
    if same_region is not None:
        probs = probs * same_region[:, None]
    probs_b = probs.astype(jnp.bfloat16)
    attended = jnp.einsum('whij,wjhd->wihd', probs_b.astype(jnp.float32), value_rows.astype(jnp.float32))
    attended_rows = attended.reshape(count, D).astype(jnp.bfloat16)
    middle_stream = residual_stream + jnp.dot(attended_rows, block_parameters[5], preferred_element_type=jnp.float32) + block_parameters[6]
    second_normalized, second_standardized, second_inverse_deviation = norm_forward(middle_stream, block_parameters[7], block_parameters[8])
    second_normalized_rows = second_normalized.astype(jnp.bfloat16)
    hidden_before_gelu = jnp.dot(second_normalized_rows, block_parameters[9], preferred_element_type=jnp.float32) + block_parameters[10]
    hidden_rows = jax.nn.gelu(hidden_before_gelu, approximate=False).astype(jnp.bfloat16)
    output = middle_stream + jnp.dot(hidden_rows, block_parameters[11], preferred_element_type=jnp.float32) + block_parameters[12]
    saved_residuals = (first_standardized, first_inverse_deviation, normalized_rows, query_rows, key_rows, value_rows, logsumexp_total, attended_rows, second_standardized, second_inverse_deviation, second_normalized_rows, hidden_before_gelu, hidden_rows)
    return (output.reshape(nwin, WIN * WIN, D), saved_residuals)

def backward_layer(grad_w, saved_residuals, block_parameters, rel_bias, same_region, one_hot):
    first_standardized, first_inverse_deviation, normalized_rows, query_rows, key_rows, value_rows, logsumexp_total, attended_rows, second_standardized, second_inverse_deviation, second_normalized_rows, hidden_before_gelu, hidden_rows = saved_residuals
    nwin = grad_w.shape[0]
    count = nwin * WIN * WIN
    scale_factor = 1.0 / math.sqrt(HEAD)
    upstream = grad_w.reshape(count, D)
    upstream_b = upstream.astype(jnp.bfloat16)
    d_reduce = jnp.dot(hidden_rows.T, upstream_b, preferred_element_type=jnp.float32)
    d_reduce_bias = lax.optimization_barrier(jnp.sum(upstream, 0))
    d_hidden = jnp.dot(upstream_b, block_parameters[11].T, preferred_element_type=jnp.float32)
    unused, pull = jax.vjp(lambda t: jax.nn.gelu(t, approximate=False), hidden_before_gelu)
    d_pre = pull(d_hidden)[0]
    d_pre_b = d_pre.astype(jnp.bfloat16)
    d_expand = jnp.dot(second_normalized_rows.T, d_pre_b, preferred_element_type=jnp.float32)
    d_expand_bias = lax.optimization_barrier(jnp.sum(d_pre, 0))
    second_norm_gradient = jnp.dot(d_pre_b, block_parameters[9].T, preferred_element_type=jnp.float32)
    backward_second, second_gain_gradient, second_offset_gradient = norm_backward(second_norm_gradient, second_standardized, second_inverse_deviation, block_parameters[7])
    grad_mid = upstream + backward_second
    grad_mid_b = grad_mid.astype(jnp.bfloat16)
    d_output = jnp.dot(attended_rows.T, grad_mid_b, preferred_element_type=jnp.float32)
    d_output_bias = lax.optimization_barrier(jnp.sum(grad_mid, 0))
    d_att = jnp.dot(grad_mid_b, block_parameters[5].T, preferred_element_type=jnp.float32).astype(jnp.bfloat16).reshape(nwin, WIN * WIN, HEADS, HEAD)
    scores = score_fn(query_rows, key_rows, rel_bias)
    probs = jnp.exp(scores - logsumexp_total)
    if same_region is not None:
        probs = probs * same_region[:, None]
    probs_b = probs.astype(jnp.bfloat16)
    d_values = jnp.einsum('whij,wihd->wjhd', probs_b.astype(jnp.float32), d_att.astype(jnp.float32))
    d_probs = jnp.einsum('wihd,wjhd->whij', d_att.astype(jnp.float32), value_rows.astype(jnp.float32))
    row_dot = lax.optimization_barrier(jnp.sum(probs * d_probs, -1, keepdims=True))
    d_scores = probs * (d_probs - row_dot)
    d_bias_map = lax.optimization_barrier(jnp.sum(d_scores, 0))
    d_table = jnp.einsum('ijt,hij->th', one_hot, d_bias_map, precision=lax.Precision.HIGHEST)
    d_scores_b = d_scores.astype(jnp.bfloat16).astype(jnp.float32)
    d_queries = jnp.einsum('whij,wjhd->wihd', d_scores_b, key_rows.astype(jnp.float32)) * scale_factor
    d_keys = jnp.einsum('whij,wihd->wjhd', d_scores_b, query_rows.astype(jnp.float32))
    d_queries = d_queries.reshape(count, D)
    d_values = d_values.reshape(count, D)
    d_qkv = jnp.concatenate([d_queries, d_keys.reshape(count, D), d_values], 1)
    d_qkv_b = d_qkv.astype(jnp.bfloat16)
    d_attend = jnp.dot(normalized_rows.T, d_qkv_b, preferred_element_type=jnp.float32)
    d_query_bias = lax.optimization_barrier(jnp.sum(d_queries, 0))
    d_value_bias = lax.optimization_barrier(jnp.sum(d_values, 0))
    normalized_gradient = jnp.dot(d_qkv_b, block_parameters[2].T, preferred_element_type=jnp.float32)
    backward_first, first_gain_gradient, first_offset_gradient = norm_backward(normalized_gradient, first_standardized, first_inverse_deviation, block_parameters[0])
    grad_in = grad_mid + backward_first
    grads = (first_gain_gradient, first_offset_gradient, d_attend, d_query_bias, d_value_bias, d_output, d_output_bias, second_gain_gradient, second_offset_gradient, d_expand, d_expand_bias, d_reduce, d_reduce_bias)
    return (grad_in.reshape(nwin, WIN * WIN, D), grads, d_table)

def reference(activations, first_gain, first_offset, attend_weight, query_bias, value_bias, output_weight, output_bias, second_gain, second_offset, expand_weight, expand_bias, reduce_weight, reduce_bias, position_table, table_index, cotangent):
    stacked = [first_gain, first_offset, attend_weight, query_bias, value_bias, output_weight, output_bias, second_gain, second_offset, expand_weight, expand_bias, reduce_weight, reduce_bias]
    params_zero = [item[0] for item in stacked]
    params_one = [item[1] for item in stacked]
    one_hot = (table_index[:, :, None] == jnp.arange(TABLE, dtype=jnp.int32)[None, None, :]).astype(jnp.float32)
    bias_zero = jnp.einsum('ijt,th->hij', one_hot, position_table[0], precision=lax.Precision.HIGHEST)
    bias_one = jnp.einsum('ijt,th->hij', one_hot, position_table[1], precision=lax.Precision.HIGHEST)
    same_region = region_select(region_labels(ROWS, 0, ROWS, COLS))

    def one_image(carry, pair):
        image, image_cot = pair
        out_zero, saved_zero = forward_layer(window_split(image[None]), params_zero, bias_zero, None)
        middle_stream = window_merge(out_zero, 1, ROWS, COLS)
        rolled = jnp.roll(middle_stream, (-SHIFT, -SHIFT), (1, 2))
        out_one, saved_one = forward_layer(window_split(rolled), params_one, bias_one, same_region)
        result = jnp.roll(window_merge(out_one, 1, ROWS, COLS), (SHIFT, SHIFT), (1, 2))
        cot_rolled = jnp.roll(image_cot[None], (-SHIFT, -SHIFT), (1, 2))
        grad_mid_w, grads_one, table_one = backward_layer(window_split(cot_rolled), saved_one, params_one, bias_one, same_region, one_hot)
        grad_mid = jnp.roll(window_merge(grad_mid_w, 1, ROWS, COLS), (SHIFT, SHIFT), (1, 2))
        grad_in_w, grads_zero, table_zero = backward_layer(window_split(grad_mid), saved_zero, params_zero, bias_zero, None, one_hot)
        grad_in = window_merge(grad_in_w, 1, ROWS, COLS)
        addend = (grads_zero, grads_one, table_zero, table_one)
        carry = jax.tree.map(lambda a, b: a + b, carry, addend)
        return (carry, (result[0], grad_in[0]))
    zero_grads = tuple((jnp.zeros(item[0].shape, jnp.float32) for item in stacked))
    start = (zero_grads, zero_grads, jnp.zeros((TABLE, HEADS), jnp.float32), jnp.zeros((TABLE, HEADS), jnp.float32))
    totals, outputs = lax.scan(one_image, start, (activations, cotangent))
    grads_zero, grads_one, table_zero, table_one = totals
    final = tuple((jnp.stack([grads_zero[i], grads_one[i]]) for i in range(13)))
    table_grad = jnp.stack([table_zero, table_one])
    return (outputs[0], outputs[1], final[0], final[1], final[2], final[3], final[4], final[5], final[6], final[7], final[8], final[9], final[10], final[11], final[12], table_grad)
```

```python
import functools
import math

import jax
import jax.numpy as jnp
from jax import lax
from jax.experimental import pallas as pl
from jax.experimental.pallas import tpu as pltpu
from jax.sharding import PartitionSpec as P

HEADS = 16
HEAD = 32
D = 512
WIN = 7
SHIFT = 3
EPS = 1e-05
SLOT = 8
ROWS_W = SLOT * SLOT
GROUP = 4
GL = GROUP * HEAD
GROUPS = HEADS // GROUP
KEYS = GROUP * ROWS_W
VEC = 16
NEG = -1e30
F32 = jnp.float32
BF16 = jnp.bfloat16


def bit_reverse(value, count):
    out = 0
    while count > 1:
        out = out * 2 + value % 2
        value //= 2
        count //= 2
    return out


def exchange(value, axis, bit):
    count = lax.axis_size(axis)
    return lax.ppermute(value, axis, [(i, i ^ bit) for i in range(count)])


def shifted(value, axis, steps):
    count = lax.axis_size(axis)
    return lax.ppermute(value, axis, [(i, (i + steps) % count) for i in range(count)])


def add_b(a, b):
    return (a.astype(F32) + b.astype(F32)).astype(BF16)


def dot(a, b):
    return lax.dot_general(a, b, (((1,), (0,)), ((), ())), preferred_element_type=F32)


def dot_nt(a, b):
    return lax.dot_general(a, b, (((1,), (1,)), ((), ())), preferred_element_type=F32)


def dot_tn(a, b):
    return lax.dot_general(a, b, (((0,), (0,)), ((), ())), preferred_element_type=F32)


def row_mask(rows):
    pos = lax.broadcasted_iota(jnp.int32, (rows, 1), 0)
    inside = ((pos % ROWS_W) < WIN * SLOT) & ((pos % SLOT) < WIN)
    return inside.astype(F32)


def chunks(columns, rolled):
    out = []
    for w in range(columns // WIN):
        for r in range(WIN):
            if not rolled:
                out.append((w, r, 0, WIN * w, WIN))
                continue
            start = WIN * w + SHIFT
            first = max(0, min(WIN, columns - start))
            if first:
                out.append((w, r, 0, start, first))
            if first < WIN:
                out.append((w, r, first, (start + first) % columns, WIN - first))
    return out


def split_windows(dst, columns, rolled, row_of):
    dst[...] = jnp.zeros(dst.shape, dst.dtype)
    for w, r, a, c, n in chunks(columns, rolled):
        ref, row = row_of(r)
        dst[pl.ds(w * ROWS_W + r * SLOT + a, n), :] = ref[row, pl.ds(c, n), :]


def merge_windows(src, columns, rolled, row_of):
    for w, r, a, c, n in chunks(columns, rolled):
        ref, row = row_of(r)
        ref[row, pl.ds(c, n), :] = src[pl.ds(w * ROWS_W + r * SLOT + a, n), :]


def standardize(values):
    centered = values - jnp.mean(values, -1, keepdims=True)
    inv = lax.rsqrt(jnp.mean(centered * centered, -1, keepdims=True) + EPS)
    return centered * inv, inv


def norm_backward(upstream, normal_x, inv, gain):
    scaled = upstream * gain
    return inv * (
        scaled
        - jnp.mean(scaled, -1, keepdims=True)
        - normal_x * jnp.mean(scaled * normal_x, -1, keepdims=True)
    )


def head_mask():
    row = lax.broadcasted_iota(jnp.int32, (KEYS, GL), 0) // ROWS_W
    lane = lax.broadcasted_iota(jnp.int32, (KEYS, GL), 1) // HEAD
    return (row == lane).astype(F32)


def group_ones():
    row = lax.broadcasted_iota(jnp.int32, (KEYS, KEYS), 0) // ROWS_W
    lane = lax.broadcasted_iota(jnp.int32, (KEYS, KEYS), 1) // ROWS_W
    return (row == lane).astype(F32).astype(BF16)


def group_sum(values, ones):
    high = values.astype(BF16)
    low = (values - high.astype(F32)).astype(BF16)
    return dot(high, ones) + dot(low, ones)


def spread(block, mask):
    return jnp.concatenate([block] * GROUP, 0) * mask


def fold(blocks, mask):
    masked = blocks * mask
    total = masked[:ROWS_W]
    for h in range(1, GROUP):
        total = total + masked[h * ROWS_W : (h + 1) * ROWS_W]
    return total


def colsum(values):
    return jnp.sum(values, 0, keepdims=True)


def place(part, shard, r, first):
    flat = (shard * first + part - first) * r
    low = part < first
    block = jnp.where(low, part, first + flat // D)
    row = jnp.where(low, shard * r, flat % D)
    return block, pl.multiple_of(row, r)


def attend_copies(meta, sources, weight, sem, r, count, store):
    out = []
    for k, source in enumerate(sources):
        core = (meta[1] % 2) ^ k
        for q in range(count):
            shard = meta[0] ^ bit_reverse(q, count)
            for t in range(2):
                here = weight.at[2 * core + t, pl.ds(pl.multiple_of(shard * r, r), r), :]
                there = source.at[q, pl.ds(t * r, r), :]
                pair = (here, there) if store else (there, here)
                out.append(pltpu.make_async_copy(*pair, sem))
    return out


def attention_forward(rolled, r, count, columns, *refs):
    meta, refs = refs[0], list(refs[1:])
    x_ref = refs.pop(0)
    halo_ref = refs.pop(0) if rolled else None
    bias_ref = refs.pop(0)
    mask_ref = refs.pop(0) if rolled else None
    a0, a1 = refs.pop(0), refs.pop(0)
    xw, mid, qkv, probs, att, vec_out = refs[:6]
    weight, vec_buf, sem, vsem = refs[6:10]
    for copy in attend_copies(meta, (a0, a1), weight, sem, r, count, False):
        copy.start()
    vec_copy = pltpu.make_async_copy(a0.at[:, pl.ds(2 * r, VEC), :], vec_buf, vsem)
    vec_copy.start()
    if rolled:
        halo = refs[10]
        halo[...] = halo_ref[...].astype(F32)
        keep = WIN - SHIFT
        split_windows(
            xw, columns, True, lambda i: (x_ref, i + SHIFT) if i < keep else (halo, i - keep)
        )
    else:
        split_windows(xw, columns, False, lambda i: (x_ref, i))
    rows = xw.shape[0]
    normal_x, _ = standardize(xw[...])
    vec_copy.wait()
    vecs = jnp.sum(vec_buf[...].astype(F32), 0)
    vec_out[...] = vecs
    normed = (normal_x * vecs[0:1] + vecs[1:2]).astype(BF16)
    pltpu.make_async_copy(weight, weight, sem).wait()
    scale = 1.0 / math.sqrt(HEAD)
    qkv[0] = ((dot(normed, weight[0]) + vecs[2:3]) * scale * row_mask(rows)).astype(BF16)
    qkv[1] = dot(normed, weight[1]).astype(BF16)
    qkv[2] = (dot(normed, weight[2]) + vecs[3:4]).astype(BF16)
    mask = head_mask().astype(BF16)
    ones = group_ones()

    def window(w, carry):
        at = pl.ds(pl.multiple_of(w * ROWS_W, ROWS_W), ROWS_W)
        for g in range(GROUPS):
            lanes = pl.ds(g * GL, GL)
            scores = dot_nt(qkv[0, at, lanes], spread(qkv[1, at, lanes], mask))
            scores = scores + bias_ref[:, pl.ds(g * KEYS, KEYS)]
            if rolled:
                scores = scores + mask_ref[w]
            total = jnp.log(group_sum(jnp.exp(scores), ones))
            prob = jnp.exp(scores - total)
            probs[g, at, :] = prob
            att[at, lanes] = dot(prob.astype(BF16), spread(qkv[2, at, lanes], mask)).astype(BF16)
        return carry

    lax.fori_loop(0, rows // ROWS_W, window, 0)
    mid[...] = xw[...] + dot(att[...], weight[3]) + vecs[4:5]


def attention_backward(rolled, r, count, columns, *refs):
    meta, gmid, xw, qkv, probs, att, vecs, vec_in, a0, a1 = refs[:10]
    refs = list(refs[10:])
    if rolled:
        stay, go = refs.pop(0), refs.pop(0)
    else:
        gin = refs.pop(0)
    dbias, keep_out, send_out = refs[:3]
    weight, grad, dqkv, datt, full, vec_buf, sem, gsem, vsem = refs[3:12]
    for copy in attend_copies(meta, (a0, a1), weight, sem, r, count, False):
        copy.start()
    rows = xw.shape[0]
    normal_x, inv = standardize(xw[...])
    gain = vecs[0:1, :]
    normed = (normal_x * gain + vecs[1:2, :]).astype(BF16)
    gm = gmid[...].astype(BF16)
    grad[3] = dot_tn(att[...], gm).astype(BF16)
    dbias[...] = jnp.zeros(dbias.shape, F32)
    mask_f = head_mask()
    mask = mask_f.astype(BF16)
    ones = group_ones()
    scale = 1.0 / math.sqrt(HEAD)
    pltpu.make_async_copy(weight, weight, sem).wait()
    datt[...] = dot_nt(gm, weight[3]).astype(BF16)

    def window(w, carry):
        at = pl.ds(pl.multiple_of(w * ROWS_W, ROWS_W), ROWS_W)
        for g in range(GROUPS):
            lanes = pl.ds(g * GL, GL)
            up = datt[at, lanes]
            prob = probs[g, at, :]
            dprob = dot_nt(up, spread(qkv[2, at, lanes], mask))
            dscore = prob * (dprob - group_sum(prob * dprob, ones))
            dbias[:, pl.ds(g * KEYS, KEYS)] += dscore
            dsb = dscore.astype(BF16)
            dqkv[0, at, lanes] = (dot(dsb, spread(qkv[1, at, lanes], mask)) * scale).astype(BF16)
            dqkv[1, at, lanes] = fold(dot_tn(dsb, qkv[0, at, lanes]), mask_f).astype(BF16)
            dqkv[2, at, lanes] = fold(dot_tn(prob.astype(BF16), up), mask_f).astype(BF16)
        return carry

    lax.fori_loop(0, rows // ROWS_W, window, 0)
    dn = jnp.zeros((rows, D), F32)
    for p in range(3):
        grad[p] = dot_tn(normed, dqkv[p]).astype(BF16)
        dn = dn + dot_nt(dqkv[p], weight[p])
    out = attend_copies(meta, (keep_out, send_out), grad, gsem, r, count, True)
    for copy in out:
        copy.start()
    dvec = jnp.concatenate(
        [
            colsum(dn * normal_x),
            colsum(dn),
            colsum(dqkv[0].astype(F32)),
            colsum(dqkv[2].astype(F32)),
        ],
        0,
    )
    vec_buf[...] = jnp.concatenate([dvec, vec_in[4:VEC, :]], 0).astype(BF16)
    vec_copies = []
    for target in (keep_out, send_out):
        for q in range(count):
            there = target.at[q, pl.ds(2 * r, VEC), :]
            vec_copies.append(pltpu.make_async_copy(vec_buf, there, vsem))
    for copy in vec_copies:
        copy.start()
    full[...] = gmid[...] + norm_backward(dn, normal_x, inv, gain)
    if rolled:
        halo = refs[12]
        keep = WIN - SHIFT
        merge_windows(full, columns, True, lambda i: (stay, i) if i < keep else (halo, i - keep))
        go[...] = halo[...].astype(BF16)
    else:
        merge_windows(full, columns, False, lambda i: (gin, i))
    for copy in vec_copies:
        copy.wait()
    for copy in out:
        copy.wait()


def mlp_copies(meta, quarters, weight, sem, r, count, store):
    out = []
    for k, source in enumerate(quarters):
        for q in range(count):
            shard = meta[0] ^ bit_reverse(q, count)
            for t in range(2):
                block, row = place(2 * (meta[1] ^ k) + t, shard, r, 4)
                here = weight.at[block, pl.ds(row, r), :]
                there = source.at[q, t]
                pair = (here, there) if store else (there, here)
                out.append(pltpu.make_async_copy(*pair, sem))
    return out


def mlp_forward(rolled, r, count, columns, *refs):
    meta, mid, vecs, c0, c1, c2, c3 = refs[:7]
    refs = list(refs[7:])
    out_a, out_b, hidden, slope = refs[:4]
    weight, full, halo, sem = refs[4:8]
    for copy in mlp_copies(meta, (c0, c1, c2, c3), weight, sem, r, count, False):
        copy.start()
    normal_x, _ = standardize(mid[...])
    normed = (normal_x * vecs[5:6, :] + vecs[6:7, :]).astype(BF16)
    full[...] = mid[...] + vecs[7:8, :]
    pltpu.make_async_copy(weight, weight, sem).wait()

    def part(p, carry):
        pre = dot(normed, weight[p]) + vecs[pl.ds(8 + p, 1), :]
        cdf = 0.5 * (1.0 + lax.erf(pre * math.sqrt(0.5)))
        hidden[p] = (pre * cdf).astype(BF16)
        density = jnp.exp(-0.5 * pre * pre) * (1.0 / math.sqrt(2.0 * math.pi))
        slope[p] = (cdf + pre * density).astype(BF16)
        full[...] += dot(hidden[p], weight[4 + p])
        return carry

    lax.fori_loop(0, 4, part, 0)
    if rolled:
        keep = WIN - SHIFT
        merge_windows(full, columns, True, lambda i: (out_a, i) if i < keep else (halo, i - keep))
        out_b[...] = halo[...].astype(BF16)
    else:
        merge_windows(full, columns, False, lambda i: (out_a, i))
        out_b[...] = out_a[:SHIFT].astype(BF16)


def mlp_backward(rolled, r, count, columns, *refs):
    meta, g_ref, halo_ref, mid, hidden, slope, vecs, c0, c1, c2, c3 = refs[:11]
    refs = list(refs[11:])
    gmid, dvec, keep_out, send_out = refs[:4]
    weight, grad, gw, halo, sem, gsem = refs[4:10]
    for copy in mlp_copies(meta, (c0, c1, c2, c3), weight, sem, r, count, False):
        copy.start()
    halo[...] = halo_ref[...].astype(F32)
    if rolled:
        keep = WIN - SHIFT
        split_windows(
            gw, columns, True, lambda i: (g_ref, i + SHIFT) if i < keep else (halo, i - keep)
        )
    else:
        split_windows(
            gw, columns, False, lambda i: (halo, i) if i < SHIFT else (g_ref, i - SHIFT)
        )
    upstream = gw[...].astype(BF16)
    normal_x, inv = standardize(mid[...])
    gain = vecs[5:6, :]
    normed = (normal_x * gain + vecs[6:7, :]).astype(BF16)
    dvec[...] = jnp.zeros(dvec.shape, F32)
    gmid[...] = jnp.zeros(gmid.shape, F32)
    pltpu.make_async_copy(weight, weight, sem).wait()

    def part(p, carry):
        grad[4 + p] = dot_tn(hidden[p], upstream).astype(BF16)
        dpre = dot_nt(upstream, weight[4 + p]) * slope[p].astype(F32)
        dvec[pl.ds(8 + p, 1), :] = colsum(dpre)
        dpb = dpre.astype(BF16)
        grad[p] = dot_tn(normed, dpb).astype(BF16)
        gmid[...] += dot_nt(dpb, weight[p])
        return carry

    lax.fori_loop(0, 4, part, 0)
    quarters = (keep_out.at[0], send_out.at[0], keep_out.at[1], send_out.at[1])
    out = mlp_copies(meta, quarters, grad, gsem, r, count, True)
    for copy in out:
        copy.start()
    dn = gmid[...]
    dvec[5:6, :] = colsum(dn * normal_x)
    dvec[6:7, :] = colsum(dn)
    dvec[7:8, :] = colsum(gw[...])
    total = gw[...] + norm_backward(dn, normal_x, inv, gain)
    gmid[...] = total
    dvec[4:5, :] = colsum(total)
    for copy in out:
        copy.wait()


def shape(dims, kind=F32):
    return jax.ShapeDtypeStruct(dims, kind)


def call(kernel, name, args, places, outs, out_places, scratch, flops):
    spec = {
        "v": pl.BlockSpec(memory_space=pltpu.VMEM),
        "s": pl.BlockSpec(memory_space=pltpu.SMEM),
        "h": pl.BlockSpec(memory_space=pl.ANY),
    }
    moved = sum(a.size * a.dtype.itemsize for a in list(args) + list(outs))
    return pl.pallas_call(
        kernel,
        name=name,
        out_shape=tuple(outs),
        in_specs=[spec[c] for c in places],
        out_specs=tuple(spec[c] for c in out_places),
        scratch_shapes=scratch,
        cost_estimate=pl.CostEstimate(flops=flops, bytes_accessed=moved, transcendentals=0),
    )(*args)


def dma():
    return pltpu.SemaphoreType.DMA


class Block:
    def __init__(self, rolled, meta, columns, r, count):
        self.rolled, self.meta = rolled, meta
        self.columns, self.r, self.count = columns, r, count
        self.rows = columns // WIN * ROWS_W
        self.fixed = (rolled, r, count, columns)

    def attend(self, x, halo, bias, mask, a0, a1):
        rows, cols = self.rows, self.columns
        args, places = [self.meta, x], "sv"
        if self.rolled:
            args.append(halo)
            places += "v"
        args.append(bias)
        places += "v"
        if self.rolled:
            args.append(mask)
            places += "v"
        args += [a0, a1]
        places += "hh"
        outs = [
            shape((rows, D)),
            shape((rows, D)),
            shape((3, rows, D), BF16),
            shape((GROUPS, rows, KEYS)),
            shape((rows, D), BF16),
            shape((VEC, D)),
        ]
        scratch = [
            pltpu.VMEM((4, D, D), BF16),
            pltpu.VMEM((self.count, VEC, D), BF16),
            dma(),
            dma(),
        ]
        if self.rolled:
            scratch.append(pltpu.VMEM((SHIFT, cols, D), F32))
        return call(
            functools.partial(attention_forward, *self.fixed),
            "attention_forward",
            args,
            places,
            outs,
            "vvvvvv",
            scratch,
            2 * rows * D * D * 6,
        )

    def attend_back(self, gmid, saved, dvec, a0, a1):
        rows, cols = self.rows, self.columns
        xw, _, qkv, probs, att, vecs = saved
        args = [self.meta, gmid, xw, qkv, probs, att, vecs, dvec, a0, a1]
        if self.rolled:
            outs = [shape((WIN - SHIFT, cols, D)), shape((SHIFT, cols, D), BF16)]
        else:
            outs = [shape((WIN, cols, D))]
        places = "v" * len(outs) + "vhh"
        packed = shape((self.count, 2 * self.r + VEC, D), BF16)
        outs += [shape((ROWS_W, HEADS * ROWS_W)), packed, packed]
        scratch = [
            pltpu.VMEM((4, D, D), BF16),
            pltpu.VMEM((4, D, D), BF16),
            pltpu.VMEM((3, rows, D), BF16),
            pltpu.VMEM((rows, D), BF16),
            pltpu.VMEM((rows, D), F32),
            pltpu.VMEM((VEC, D), BF16),
            dma(),
            dma(),
            dma(),
        ]
        if self.rolled:
            scratch.append(pltpu.VMEM((SHIFT, cols, D), F32))
        return call(
            functools.partial(attention_backward, *self.fixed),
            "attention_backward",
            args,
            "svvvvvvvhh",
            outs,
            places,
            scratch,
            2 * rows * D * D * 14,
        )

    def mlp(self, mid, vecs, quarters):
        rows, cols = self.rows, self.columns
        first = WIN - SHIFT if self.rolled else WIN
        outs = [
            shape((first, cols, D)),
            shape((SHIFT, cols, D), BF16),
            shape((4, rows, D), BF16),
            shape((4, rows, D), BF16),
        ]
        scratch = [
            pltpu.VMEM((8, D, D), BF16),
            pltpu.VMEM((rows, D), F32),
            pltpu.VMEM((SHIFT, cols, D), F32),
            dma(),
        ]
        return call(
            functools.partial(mlp_forward, *self.fixed),
            "mlp_forward",
            [self.meta, mid, vecs, *quarters],
            "svvhhhh",
            outs,
            "vvvv",
            scratch,
            2 * rows * D * D * 8,
        )

    def mlp_back(self, g, halo, mid, hidden, slope, vecs, quarters):
        rows, cols = self.rows, self.columns
        packed = shape((2, self.count, 2, self.r, D), BF16)
        outs = [shape((rows, D)), shape((VEC, D)), packed, packed]
        scratch = [
            pltpu.VMEM((8, D, D), BF16),
            pltpu.VMEM((8, D, D), BF16),
            pltpu.VMEM((rows, D), F32),
            pltpu.VMEM((SHIFT, cols, D), F32),
            dma(),
            dma(),
        ]
        return call(
            functools.partial(mlp_backward, *self.fixed),
            "mlp_backward",
            [self.meta, g, halo, mid, hidden, slope, vecs, *quarters],
            "svvvvvvhhhh",
            outs,
            "vvhh",
            scratch,
            2 * rows * D * D * 16,
        )


def gather_fsdp(value):
    bit = lax.axis_size("fsdp") // 2
    while bit:
        value = jnp.concatenate([value, exchange(value, "fsdp", bit)], 0)
        bit //= 2
    return value


def scatter_fsdp(keep, got):
    bit = 1
    count = lax.axis_size("fsdp")
    while bit < count:
        half = keep.shape[0] // 2
        send = keep[half:] if got is None else add_b(keep[half:], got[half:])
        mine = keep[:half] if got is None else add_b(keep[:half], got[:half])
        keep, got = mine, exchange(send, "fsdp", bit)
        bit *= 2
    return keep, got


def columns_apart(matrix):
    rows, width = matrix.shape
    return matrix.reshape(rows, width // D, D).transpose(1, 0, 2)


def place_vectors(rows_list, wide, fsdp, count):
    part = D // count
    lane = jnp.arange(D, dtype=jnp.int32)
    narrow = jnp.stack(rows_list)
    narrow = jnp.where((lane // part == fsdp)[None], jnp.tile(narrow, (1, count)), 0.0)
    total = wide.shape[0] * count
    spot = jnp.arange(total, dtype=jnp.int32)
    wide = jnp.where(spot // wide.shape[0] == fsdp, jnp.tile(wide, (count,)), 0.0)
    wide = wide.reshape(total // D, D)
    rest = jnp.zeros((VEC - narrow.shape[0] - wide.shape[0], D), F32)
    return jnp.concatenate([narrow, wide, rest], 0).astype(BF16)


def window_pad(table, fill):
    side = table.reshape(WIN, WIN, WIN, WIN)
    side = jnp.pad(side, ((0, 1), (0, 1), (0, 1), (0, 1)), constant_values=fill)
    return side.reshape(ROWS_W, ROWS_W)


def slice_label(positions, total):
    first = (positions >= total - WIN).astype(jnp.int32)
    second = (positions >= total - SHIFT).astype(jnp.int32)
    return first + second


def body(
    activations,
    first_gain,
    first_offset,
    attend_weight,
    query_bias,
    value_bias,
    output_weight,
    output_bias,
    second_gain,
    second_offset,
    expand_weight,
    expand_bias,
    reduce_weight,
    reduce_bias,
    position_table,
    table_index,
    cotangent,
):
    count = lax.axis_size("fsdp")
    bands = lax.axis_size("seq")
    fsdp = lax.axis_index("fsdp")
    seq = lax.axis_index("seq")
    core = seq % 2
    batch, band_rows, columns, _ = activations.shape
    assert batch == 1 and band_rows == WIN and bands == 4
    r = attend_weight.shape[1]
    meta = jnp.stack([fsdp, seq]).astype(jnp.int32)

    cot = cotangent[0]
    cot_halo = shifted(cot[:SHIFT].astype(BF16), "seq", -1)

    weights_a, weights_c = [], []
    for l in range(2):
        vectors = place_vectors(
            [
                first_gain[l],
                first_offset[l],
                query_bias[l],
                value_bias[l],
                output_bias[l],
                second_gain[l],
                second_offset[l],
                reduce_bias[l],
            ],
            expand_bias[l],
            fsdp,
            count,
        )
        parts = jnp.concatenate([columns_apart(attend_weight[l]), output_weight[l][None]], 0)
        half = jnp.where(core == 0, parts[:2], parts[2:]).reshape(1, 2 * r, D)
        own_a = jnp.concatenate([half, vectors[None]], 1)
        expand = columns_apart(expand_weight[l])
        reduce = reduce_weight[l].reshape(4, r, D)
        lower = jnp.where(core == 0, expand[:2], expand[2:])
        upper = jnp.where(core == 0, reduce[:2], reduce[2:])
        own_c = jnp.where(seq < 2, lower, upper)[None]
        c0 = gather_fsdp(own_c)
        a0 = gather_fsdp(own_a)
        c2 = exchange(c0, "seq", 2)
        c1 = exchange(c0, "seq", 1)
        a1 = exchange(a0, "seq", 1)
        c3 = exchange(c2, "seq", 1)
        weights_a.append((a0, a1))
        weights_c.append((c0, c1, c2, c3))

    table_rows = position_table.shape[1]
    padded = window_pad(table_index, -1)
    one_hot = (padded[:, :, None] == jnp.arange(table_rows, dtype=jnp.int32)).astype(F32)
    pad_keys = jnp.where(padded[0] < 0, NEG, 0.0).astype(F32)
    biases = []
    for l in range(2):
        bias = jnp.einsum(
            "ijt,th->ihj", one_hot, position_table[l], precision=lax.Precision.HIGHEST
        )
        biases.append((bias + pad_keys[None, None, :]).reshape(ROWS_W, HEADS * ROWS_W))

    row_lab = slice_label(seq * band_rows + jnp.arange(band_rows), band_rows * bands)
    col_lab = slice_label(jnp.arange(columns), columns).reshape(columns // WIN, WIN)
    labels = row_lab[None, :, None] * 3 + col_lab[:, None, :]
    labels = jnp.pad(labels, ((0, 0), (0, 1), (0, 1))).reshape(columns // WIN, ROWS_W)
    apart = labels[:, :, None] != labels[:, None, :]
    mask = jnp.where(apart & (padded >= 0)[None], NEG, 0.0).astype(F32)
    mask = jnp.tile(mask, (1, 1, GROUP))

    zero = Block(False, meta, columns, r, count)
    one = Block(True, meta, columns, r, count)

    saved_zero = zero.attend(activations[0], None, biases[0], None, *weights_a[0])
    out_zero, top, hid_zero, slope_zero = zero.mlp(saved_zero[1], saved_zero[5], weights_c[0])
    halo = shifted(top, "seq", -1)
    saved_one = one.attend(out_zero, halo, biases[1], mask, *weights_a[1])
    stay, go, hid_one, slope_one = one.mlp(saved_one[1], saved_one[5], weights_c[1])
    block_output = jnp.concatenate([shifted(go, "seq", 1).astype(F32), stay], 0)[None]

    gmid, dvec, keep_c1, send_c1 = one.mlp_back(
        cot, cot_halo, saved_one[1], hid_one, slope_one, saved_one[5], weights_c[1]
    )
    stay, go, dbias_one, keep_a1, send_a1 = one.attend_back(gmid, saved_one, dvec, *weights_a[1])
    halo = shifted(go, "seq", 1)
    gmid, dvec, keep_c0, send_c0 = zero.mlp_back(
        stay, halo, saved_zero[1], hid_zero, slope_zero, saved_zero[5], weights_c[0]
    )
    grad_in, dbias_zero, keep_a0, send_a0 = zero.attend_back(
        gmid, saved_zero, dvec, *weights_a[0]
    )

    tables = []
    for dbias in (dbias_zero, dbias_one):
        grid = dbias.reshape(ROWS_W, HEADS, ROWS_W)
        tables.append(
            jnp.einsum("ijt,ihj->th", one_hot, grid, precision=lax.Precision.HIGHEST)
        )
    table_grad = lax.psum(jnp.stack(tables), ("seq", "fsdp"))

    grads = []
    for keep_a, send_a, keep_c, send_c in (
        (keep_a0, send_a0, keep_c0, send_c0),
        (keep_a1, send_a1, keep_c1, send_c1),
    ):
        got = exchange(send_c, "seq", 1)
        got_y = exchange(add_b(keep_c[1], got[1]), "seq", 2)
        mine = add_b(keep_c[0], got[0])
        own = add_b(*scatter_fsdp(mine, got_y))[0]
        pair = jnp.stack([own, exchange(own, "seq", 2)])
        other = exchange(pair, "seq", 1)
        even = jnp.where(core == 0, pair, other)
        odd = jnp.where(core == 0, other, pair)
        flip = seq < 2
        both = jnp.concatenate([even, odd], 1)
        low = jnp.where(flip, both[0], both[1])
        high = jnp.where(flip, both[1], both[0])
        d_expand = low.transpose(1, 0, 2).reshape(r, 4 * D).astype(F32)
        d_reduce = high.reshape(4 * r, D).astype(F32)

        got = exchange(send_a, "seq", 1)
        own = add_b(*scatter_fsdp(keep_a, got))[0]
        own = add_b(own, exchange(own, "seq", 2))
        matrix = own[: 2 * r].reshape(2, r, D)
        other = exchange(matrix, "seq", 1)
        even = jnp.where(core == 0, matrix, other)
        odd = jnp.where(core == 0, other, matrix)
        d_attend = jnp.concatenate([even[0], even[1], odd[0]], 1).astype(F32)
        d_output = odd[1].astype(F32)
        vecs = own[2 * r :].astype(F32)
        part = D // count
        narrow = lax.dynamic_slice(vecs, (0, fsdp * part), (8, part))
        wide = lax.dynamic_slice(vecs[8:12].reshape(4 * D), (fsdp * 4 * part,), (4 * part,))
        grads.append(
            (
                narrow[0],
                narrow[1],
                d_attend,
                narrow[2],
                narrow[3],
                d_output,
                narrow[4],
                narrow[5],
                narrow[6],
                d_expand,
                wide,
                d_reduce,
                narrow[7],
            )
        )
    final = [jnp.stack([a, b]) for a, b in zip(*grads)]
    return tuple([block_output, grad_in[None]] + final + [table_grad])


def solution(mesh):
    vector = P(None, "fsdp")
    matrix = P(None, "fsdp", None)
    image = P("fsdp", "seq", None, None)
    params = (
        vector,
        vector,
        matrix,
        vector,
        vector,
        matrix,
        vector,
        vector,
        vector,
        matrix,
        vector,
        matrix,
        vector,
    )
    return jax.shard_map(
        body,
        mesh=mesh,
        in_specs=(image, *params, P(), P(), image),
        out_specs=(image, image, *params, P()),
        check_vma=False,
    )
```
